32 devices in a mesh: grp: 2 (over y), lon: 4 (over z), view: 4 (over x, core).
Axes of the slice: x: 2, y: 2, z: 4, core: 2. Of those that a mesh axis runs over, the one named last changes fastest.
Arguments:
- light_field: bfloat16 [128, 4, 128, 128], P(('grp', 'view'), None, 'lon'), parts along dimension 0, may hold values from -6 to 6
- spatial_weights: bfloat16 [3, 3, 3, 128, 128], replicated, may hold values from -0.1875 to 0.1875
- spatial_offsets: float32 [3, 128], replicated, may hold values from -3 to 3
- angular_weight: bfloat16 [3, 3, 128, 128], replicated, may hold values from -0.1875 to 0.1875
- angular_offset: float32 [128], replicated, may hold values from -3 to 3
Outputs:
- refined: bfloat16 [128, 4, 128, 128], P(('grp', 'view'), None, 'lon'), parts along dimension 0
The draws below stay inside these ranges and needn't reach their ends.
There are 2 independent parts, one for each index of `grp`. The reference program is written for one: setup_inputs(seed, part) draws one part's arguments, and reference() takes and returns one part's arrays. A program takes and returns all parts, laid end to end along the dimension named above; an argument that names none is the same for every part. Nothing has to cross between parts.
All inputs are finite; a program needn't handle non-finite values.
Results may differ from the reference program's by a relative error of at most 0.0047.
Values may be sent and summed in bfloat16 or wider, within the bound.
A program may use at most 64 MiB of HBM per device.

```python
import jax
import jax.numpy as jnp
from jax import lax

C = 128
ANG = 8
LAYERS = 3
VIEWS = 64
ROWS = 4
COLS = 128


def shard_levels(key, extent, shards, smallest, high):
    def one(position, blocks):
        draws = jax.random.uniform(jax.random.fold_in(jax.random.fold_in(key, 6), position), (blocks,), jnp.float32, smallest / len(shards), high / len(shards))
        return jnp.repeat(jnp.exp(draws), extent[position] // blocks).reshape((-1,) + (1,) * (len(extent) - position - 1))

    level = one(*shards[0])
    for cut in shards[1:]:
        level = level * one(*cut)
    return level


def gaussian(own_key, dims, deviation, limit, cuts=(), held_as=jnp.bfloat16):
    entries = deviation * jax.random.normal(own_key, dims, jnp.float32)
    if cuts:
        entries = entries * shard_levels(own_key, dims, cuts, -0.22, 0.18)
    return jnp.clip(entries, -limit, limit).astype(held_as)


def setup_inputs(seed: int = 0, part: int = 0) -> dict:
    seeds = jax.random.split(jax.random.key(seed), 6)
    part_splits = jax.random.split(jax.random.fold_in(seeds[5], part), 6)
    light_field = gaussian(part_splits[0], (VIEWS, ROWS, COLS, C), 1.0, 6.0, ((0, 4), (2, 4)))
    spatial_weights = gaussian(seeds[1], (LAYERS, 3, 3, C, C), (9 * C) ** -0.5, 0.1875)
    spatial_offsets = gaussian(seeds[2], (LAYERS, C), 0.5, 3.0, (), jnp.float32)
    angular_weight = gaussian(seeds[3], (3, 3, C, C), (9 * C) ** -0.5, 0.1875)
    angular_offset = gaussian(seeds[4], (C,), 0.5, 3.0, (), jnp.float32)
    return {"light_field": light_field, "spatial_weights": spatial_weights, "spatial_offsets": spatial_offsets, "angular_weight": angular_weight, "angular_offset": angular_offset}


def spatial_layer(hidden, weight, offset):
    rows, cols, chans = hidden.shape
    padded = jnp.pad(hidden, ((1, 1), (0, 0), (0, 0)))
    padded = jnp.concatenate([padded[:, -1:], padded, padded[:, :1]], axis=1)
    total = jnp.zeros((rows * cols, chans), jnp.float32)
    for row_tap in range(3):
        for col_tap in range(3):
            window = padded[row_tap:row_tap + rows, col_tap:col_tap + cols].reshape(-1, chans)
            total = total + jnp.dot(window, weight[row_tap, col_tap], preferred_element_type=jnp.float32)
    total = total.reshape(rows, cols, chans) + offset
    return jax.nn.gelu(total, approximate=True).astype(jnp.bfloat16)


def reference(light_field, spatial_weights, spatial_offsets, angular_weight, angular_offset):
    hidden = light_field
    for layer_index in range(LAYERS):
        weight = spatial_weights[layer_index]
        offset = spatial_offsets[layer_index]
        hidden = lax.map(lambda single: spatial_layer(single, weight, offset), hidden)
    chans = hidden.shape[-1]
    views_grid = hidden.reshape(ANG, ANG, -1, chans)
    padded = jnp.pad(views_grid, ((1, 1), (1, 1), (0, 0), (0, 0)))
    total = jnp.zeros((views_grid.shape[0] * ANG * views_grid.shape[2], chans), jnp.float32)
    for row_tap in range(3):
        for col_tap in range(3):
            window = padded[row_tap:row_tap + ANG, col_tap:col_tap + ANG].reshape(-1, chans)
            total = total + jnp.dot(window, angular_weight[row_tap, col_tap], preferred_element_type=jnp.float32)
    angular = (total + angular_offset).astype(jnp.bfloat16)
    angular = lax.optimization_barrier(angular).reshape(light_field.shape)
    return (light_field.astype(jnp.float32) + angular.astype(jnp.float32)).astype(jnp.bfloat16)
```

```python
import functools

import jax
import jax.numpy as jnp
from jax import lax
from jax.experimental import pallas as pl
from jax.experimental.pallas import tpu as pltpu
from jax.sharding import PartitionSpec as P

ANG = 8
F32 = jnp.float32
BF16 = jnp.bfloat16


def gelu(t):
    return 0.5 * t * (1.0 + jnp.tanh(0.7978845608 * (t + 0.044715 * (t * t * t))))


def kernel(lon_count, view_count, lf, sw, so, aw, ao, out, lfv, x0, x1, x2, flip, hid, wide, awide, acc,
           in_sem, w_sem, lon_send, lon_recv, view_send, view_recv):
    views, rows, cols, chans = lf.shape
    layers = sw.shape[0]
    grid_rows = views // ANG
    pairs = rows // 2
    lon = lax.axis_index("lon")
    view = lax.axis_index("view")
    right, left = lax.rem(lon + 1, lon_count), lax.rem(lon + lon_count - 1, lon_count)
    has_low, has_high = view > 0, view < view_count - 1

    loads = [pltpu.make_async_copy(lf.at[:, r], lfv.at[:, r], in_sem.at[r]) for r in range(rows)]
    for load in loads:
        load.start()
    weights = []
    for l in range(layers):
        weights.append((
            pltpu.make_async_copy(sw.at[l], wide.at[l, 0:3, :, :, 0:chans], w_sem.at[l, 0]),
            pltpu.make_async_copy(sw.at[l], wide.at[l, 1:4, :, :, chans:2 * chans], w_sem.at[l, 1]),
        ))
    weights.append((
        pltpu.make_async_copy(aw, awide.at[:, 0:3, :, 0:chans], w_sem.at[layers, 0]),
        pltpu.make_async_copy(aw, awide.at[:, 1:4, :, chans:2 * chans], w_sem.at[layers, 1]),
    ))
    for both in weights:
        for copy in both:
            copy.start()

    barrier = pltpu.get_barrier_semaphore()
    for neighbour in (left, right):
        pl.semaphore_signal(barrier, inc=1, device_id={"lon": neighbour}, device_id_type=pl.DeviceIdType.MESH)

    @pl.when(has_low)
    def _():
        pl.semaphore_signal(barrier, inc=1, device_id={"view": view - 1}, device_id_type=pl.DeviceIdType.MESH)

    @pl.when(has_high)
    def _():
        pl.semaphore_signal(barrier, inc=1, device_id={"view": view + 1}, device_id_type=pl.DeviceIdType.MESH)

    blank = jnp.zeros((3, chans, chans), BF16)
    for l in range(layers):
        wide[l, 0, :, :, chans:2 * chans] = blank
        wide[l, 3, :, :, 0:chans] = blank
    awide[:, 0, :, chans:2 * chans] = blank
    awide[:, 3, :, 0:chans] = blank

    @pl.when(jnp.logical_not(has_low))
    def _():
        hid[0] = jnp.zeros(hid.shape[1:], BF16)

    @pl.when(jnp.logical_not(has_high))
    def _():
        hid[grid_rows + 1] = jnp.zeros(hid.shape[1:], BF16)

    for r in range(rows):
        loads[r].wait()
        for v in range(views):
            flip[r, pl.ds(v, cols, stride=views), :] = lfv[v, r].astype(F32)
        x0[r, 3 * views:(cols + 3) * views, :] = flip[r].astype(BF16)

    pl.semaphore_wait(barrier, 2 + has_low.astype(jnp.int32) + has_high.astype(jnp.int32))
    to_left = pltpu.make_async_remote_copy(
        src_ref=x0.at[:, 3 * views:6 * views], dst_ref=x0.at[:, (cols + 3) * views:(cols + 6) * views],
        send_sem=lon_send.at[0], recv_sem=lon_recv.at[0],
        device_id={"lon": left}, device_id_type=pl.DeviceIdType.MESH)
    to_right = pltpu.make_async_remote_copy(
        src_ref=x0.at[:, cols * views:(cols + 3) * views], dst_ref=x0.at[:, 0:3 * views],
        send_sem=lon_send.at[1], recv_sem=lon_recv.at[1],
        device_id={"lon": right}, device_id_type=pl.DeviceIdType.MESH)
    to_left.start()
    to_right.start()

    def layer(l, src, p, spans):
        low = max(2 * p - 1, 0)
        high = min(2 * p + 3, rows)
        first, last = low - (2 * p - 1), high - (2 * p - 1)
        taps = []
        for row in range(low, high):
            for b in range(3):
                pieces = [src[row, (s + b) * views:(e + b) * views, :] for s, e in spans]
                taps.append(pieces[0] if len(pieces) == 1 else jnp.concatenate(pieces, axis=0))
        stacked = jnp.concatenate(taps, axis=1)
        weight = wide[l, first:last].reshape((last - first) * 3 * chans, 2 * chans)
        total = jnp.dot(stacked, weight, preferred_element_type=F32)
        offset = so[l:l + 1, :]
        return [gelu(total[:, h * chans:(h + 1) * chans] + offset) for h in range(2)]

    for copy in weights[0]:
        copy.wait()
    for p in range(pairs):
        for h, value in enumerate(layer(0, x0, p, ((3, cols + 1),))):
            x1[2 * p + h, 3 * views:(cols + 1) * views, :] = value.astype(BF16)
    to_left.wait()
    to_right.wait()
    for p in range(pairs):
        for h, value in enumerate(layer(0, x0, p, ((0, 3), (cols + 1, cols + 4)))):
            value = value.astype(BF16)
            x1[2 * p + h, 0:3 * views, :] = value[:3 * views]
            x1[2 * p + h, (cols + 1) * views:(cols + 4) * views, :] = value[3 * views:]
    for copy in weights[1]:
        copy.wait()
    for p in range(pairs):
        for h, value in enumerate(layer(1, x1, p, ((0, cols + 2),))):
            x2[2 * p + h] = value.astype(BF16)
    for copy in weights[2]:
        copy.wait()

    ups, downs = [], []
    for p in range(pairs):
        for h, value in enumerate(layer(2, x2, p, ((0, cols),))):
            r = 2 * p + h
            flip[r] = value
            for v in range(views):
                hid[1 + v // ANG, v % ANG, r * cols:(r + 1) * cols, :] = (
                    flip[r, pl.ds(v, cols, stride=views), :].astype(BF16))
        span = slice(2 * p * cols, (2 * p + 2) * cols)
        ups.append(pltpu.make_async_remote_copy(
            src_ref=hid.at[grid_rows, :, span], dst_ref=hid.at[0, :, span],
            send_sem=view_send.at[0, p], recv_sem=view_recv.at[0, p],
            device_id={"view": view + 1}, device_id_type=pl.DeviceIdType.MESH))
        downs.append(pltpu.make_async_remote_copy(
            src_ref=hid.at[1, :, span], dst_ref=hid.at[grid_rows + 1, :, span],
            send_sem=view_send.at[1, p], recv_sem=view_recv.at[1, p],
            device_id={"view": view - 1}, device_id_type=pl.DeviceIdType.MESH))

        @pl.when(has_high)
        def _(copy=ups[-1]):
            copy.start()

        @pl.when(has_low)
        def _(copy=downs[-1]):
            copy.start()

    for copy in weights[3]:
        copy.wait()

    def partial(u, q, near):
        lo, hi = max(2 * q - 1, 0), min(2 * q + 3, ANG)
        first, last = lo - (2 * q - 1), hi - (2 * q - 1)
        lhs, rhs = [], []
        for a in range(3):
            if (1 <= u + a <= grid_rows) != near:
                continue
            lhs.extend(hid[u + a, v] for v in range(lo, hi))
            rhs.append(awide[a, first:last].reshape((last - first) * chans, 2 * chans))
        return jnp.dot(jnp.concatenate(lhs, axis=1), jnp.concatenate(rhs, axis=0), preferred_element_type=F32)

    for u in range(grid_rows):
        for q in range(ANG // 2):
            acc[u, q] = partial(u, q, True)

    @pl.when(has_low)
    def _():
        for copy in ups:
            copy.wait_recv()

    @pl.when(has_high)
    def _():
        for copy in downs:
            copy.wait_recv()

    offset = ao[...]
    for u in range(grid_rows):
        for q in range(ANG // 2):
            total = acc[u, q]
            if u == 0 or u == grid_rows - 1:
                total = total + partial(u, q, False)
            for h in range(2):
                v = u * ANG + 2 * q + h
                angular = (total[:, h * chans:(h + 1) * chans] + offset).astype(BF16).astype(F32)
                own = lfv[v].reshape(rows * cols, chans).astype(F32)
                out[v] = (own + angular).astype(BF16).reshape(rows, cols, chans)

    @pl.when(has_high)
    def _():
        for copy in ups:
            copy.wait_send()

    @pl.when(has_low)
    def _():
        for copy in downs:
            copy.wait_send()


def local(lon_count, view_count, lf, sw, so, aw, ao):
    views, rows, cols, chans = lf.shape
    layers = sw.shape[0]
    grid_rows = views // ANG
    pairs = rows // 2
    hbm = pl.BlockSpec(memory_space=pl.ANY)
    vmem = pl.BlockSpec(memory_space=pltpu.VMEM)
    return pl.pallas_call(
        functools.partial(kernel, lon_count, view_count),
        out_shape=jax.ShapeDtypeStruct(lf.shape, BF16),
        in_specs=[hbm, hbm, vmem, hbm, vmem],
        out_specs=vmem,
        scratch_shapes=[
            pltpu.VMEM(lf.shape, BF16),
            pltpu.VMEM((rows, (cols + 6) * views, chans), BF16),
            pltpu.VMEM((rows, (cols + 4) * views, chans), BF16),
            pltpu.VMEM((rows, (cols + 2) * views, chans), BF16),
            pltpu.VMEM((rows, cols * views, chans), F32),
            pltpu.VMEM((grid_rows + 2, ANG, rows * cols, chans), BF16),
            pltpu.VMEM((layers, 4, 3, chans, 2 * chans), BF16),
            pltpu.VMEM((3, 4, chans, 2 * chans), BF16),
            pltpu.VMEM((grid_rows, ANG // 2, rows * cols, 2 * chans), F32),
            pltpu.SemaphoreType.DMA((rows,)),
            pltpu.SemaphoreType.DMA((layers + 1, 2)),
            pltpu.SemaphoreType.DMA((2,)),
            pltpu.SemaphoreType.DMA((2,)),
            pltpu.SemaphoreType.DMA((2, pairs)),
            pltpu.SemaphoreType.DMA((2, pairs)),
        ],
        compiler_params=pltpu.CompilerParams(collective_id=0, has_side_effects=True),
    )(lf, sw, so, aw, ao.reshape(1, chans))


def solution(mesh):
    return jax.shard_map(
        functools.partial(local, mesh.shape["lon"], mesh.shape["view"]),
        mesh=mesh,
        in_specs=(P(("grp", "view"), None, "lon", None), P(), P(), P(), P()),
        out_specs=P(("grp", "view"), None, "lon", None),
        check_vma=False,
    )
```

```python
import functools

import jax
import jax.numpy as jnp
from jax import lax
from jax.experimental import pallas as pl
from jax.experimental.pallas import tpu as pltpu
from jax.sharding import PartitionSpec as P

ANG = 8
EDGE = 4
F32 = jnp.float32
BF16 = jnp.bfloat16


def gelu(t):
    return 0.5 * t * (1.0 + jnp.tanh(0.7978845608 * (t + 0.044715 * (t * t * t))))


def kernel(lon_count, view_count, lf, sw, so_hbm, aw, ao_hbm, out, so, ao, lfv, x0, x1, x2, flip, flip_edge, hid, hid_edge, wide, awide,
           acc, acc_edge, full,
           in_sem, w_sem, b_sem, lon_send, lon_recv, view_send, view_recv):
    views, rows, cols, chans = lf.shape
    layers = sw.shape[0]
    grid_rows = views // ANG
    pairs = rows // 2
    lon = lax.axis_index("lon")
    view = lax.axis_index("view")
    right, left = lax.rem(lon + 1, lon_count), lax.rem(lon + lon_count - 1, lon_count)
    has_low, has_high = view > 0, view < view_count - 1

    barrier = pltpu.get_barrier_semaphore()
    for neighbour in (left, right):
        pl.semaphore_signal(barrier, inc=1, device_id={"lon": neighbour}, device_id_type=pl.DeviceIdType.MESH)

    @pl.when(has_low)
    def _():
        pl.semaphore_signal(barrier, inc=1, device_id={"view": view - 1}, device_id_type=pl.DeviceIdType.MESH)

    @pl.when(has_high)
    def _():
        pl.semaphore_signal(barrier, inc=1, device_id={"view": view + 1}, device_id_type=pl.DeviceIdType.MESH)

    loads = [pltpu.make_async_copy(lf.at[:, r], lfv.at[:, r], in_sem.at[r]) for r in range(rows)]
    for load in loads:
        load.start()
    biases = [pltpu.make_async_copy(so_hbm, so, b_sem.at[0]), pltpu.make_async_copy(ao_hbm, ao, b_sem.at[1])]
    for copy in biases:
        copy.start()
    weights = []
    for l in range(layers):
        weights.append((
            pltpu.make_async_copy(sw.at[l], wide.at[l, 0:3, :, :, 0:chans], w_sem.at[l, 0]),
            pltpu.make_async_copy(sw.at[l], wide.at[l, 1:4, :, :, chans:2 * chans], w_sem.at[l, 1]),
        ))
    weights.append((
        pltpu.make_async_copy(aw, awide.at[:, 0:3, :, 0:chans], w_sem.at[layers, 0]),
        pltpu.make_async_copy(aw, awide.at[:, 1:4, :, chans:2 * chans], w_sem.at[layers, 1]),
    ))
    for both in weights:
        for copy in both:
            copy.start()

    blank = jnp.zeros((3, chans, chans), BF16)
    for l in range(layers):
        wide[l, 0, :, :, chans:2 * chans] = blank
        wide[l, 3, :, :, 0:chans] = blank
    awide[:, 0, :, chans:2 * chans] = blank
    awide[:, 3, :, 0:chans] = blank

    @pl.when(jnp.logical_not(has_low))
    def _():
        hid[0] = jnp.zeros(hid.shape[1:], BF16)
        hid_edge[0] = jnp.zeros(hid_edge.shape[1:], BF16)

    @pl.when(jnp.logical_not(has_high))
    def _():
        hid[grid_rows + 1] = jnp.zeros(hid.shape[1:], BF16)
        hid_edge[grid_rows + 1] = jnp.zeros(hid_edge.shape[1:], BF16)

    for x in (x0, x1, x2):
        x[0] = jnp.zeros(x.shape[1:], BF16)
        x[rows + 1] = jnp.zeros(x.shape[1:], BF16)

    for r in range(rows):
        loads[r].wait()
        for v in range(views):
            flip[r, pl.ds(v, cols, stride=views), :] = lfv[v, r].astype(F32)
        x0[r + 1, 3 * views:(cols + 3) * views, :] = flip[r].astype(BF16)

    def activate(l, total):
        offset = so[l:l + 1, :]
        return [gelu(total[:, h * chans:(h + 1) * chans] + offset) for h in range(2)]

    def inner(l, src, p, start, end):
        low, high = max(2 * p, 1), min(2 * p + 4, rows + 1)
        first, last = low - 2 * p, high - 2 * p
        taps = [src[row, (start + b) * views:(end + b) * views, :] for row in range(low, high) for b in range(3)]
        weight = wide[l, first:last].reshape((last - first) * 3 * chans, 2 * chans)
        return activate(l, jnp.dot(jnp.concatenate(taps, axis=1), weight, preferred_element_type=F32))

    def outer(l, src, spans):
        taps = []
        for i in range(4):
            for b in range(3):
                taps.append(jnp.concatenate(
                    [src[2 * p + i, (s + b) * views:(e + b) * views, :] for p in range(pairs) for s, e in spans], axis=0))
        weight = wide[l].reshape(12 * chans, 2 * chans)
        return activate(l, jnp.dot(jnp.concatenate(taps, axis=1), weight, preferred_element_type=F32))

    def store_outer(dst, values, width):
        side = 3 * views
        for h, value in enumerate(values):
            value = value.astype(BF16)
            for p in range(pairs):
                dst[2 * p + h + 1, 0:side, :] = value[2 * p * side:(2 * p + 1) * side]
                dst[2 * p + h + 1, (width - 3) * views:width * views, :] = value[(2 * p + 1) * side:(2 * p + 2) * side]

    def view_copies(ref, k, span):
        up = pltpu.make_async_remote_copy(
            src_ref=ref.at[grid_rows, :, span], dst_ref=ref.at[0, :, span],
            send_sem=view_send.at[0, k], recv_sem=view_recv.at[0, k],
            device_id={"view": view + 1}, device_id_type=pl.DeviceIdType.MESH)
        down = pltpu.make_async_remote_copy(
            src_ref=ref.at[1, :, span], dst_ref=ref.at[grid_rows + 1, :, span],
            send_sem=view_send.at[1, k], recv_sem=view_recv.at[1, k],
            device_id={"view": view - 1}, device_id_type=pl.DeviceIdType.MESH)

        @pl.when(has_high)
        def _():
            up.start()

        @pl.when(has_low)
        def _():
            down.start()

        return up, down

    def receive(copies):
        @pl.when(has_low)
        def _():
            for up, _ in copies:
                up.wait_recv()

        @pl.when(has_high)
        def _():
            for _, down in copies:
                down.wait_recv()

    for copy in biases:
        copy.wait()
    for copy in weights[0]:
        copy.wait()
    for p in range(pairs):
        for h, value in enumerate(inner(0, x0, p, 3, cols + 1)):
            x1[2 * p + h + 1, 3 * views:(cols + 1) * views, :] = value.astype(BF16)
    for copy in weights[1]:
        copy.wait()
    for p in range(pairs):
        for h, value in enumerate(inner(1, x1, p, 3, cols - 1)):
            x2[2 * p + h + 1, 3 * views:(cols - 1) * views, :] = value.astype(BF16)

    pl.semaphore_wait(barrier, 2 + has_low.astype(jnp.int32) + has_high.astype(jnp.int32))
    to_left = pltpu.make_async_remote_copy(
        src_ref=x0.at[1:rows + 1, 3 * views:6 * views],
        dst_ref=x0.at[1:rows + 1, (cols + 3) * views:(cols + 6) * views],
        send_sem=lon_send.at[0], recv_sem=lon_recv.at[0],
        device_id={"lon": left}, device_id_type=pl.DeviceIdType.MESH)
    to_right = pltpu.make_async_remote_copy(
        src_ref=x0.at[1:rows + 1, cols * views:(cols + 3) * views], dst_ref=x0.at[1:rows + 1, 0:3 * views],
        send_sem=lon_send.at[1], recv_sem=lon_recv.at[1],
        device_id={"lon": right}, device_id_type=pl.DeviceIdType.MESH)
    to_left.start()
    to_right.start()

    for copy in weights[2]:
        copy.wait()
    middle = cols - 2 * EDGE
    sent = []
    for p in range(pairs):
        for h, value in enumerate(inner(2, x2, p, EDGE, cols - EDGE)):
            flip[2 * p + h, 0:middle * views] = value
        for v in range(views):
            both = [flip[2 * p + h, pl.ds(v, middle, stride=views), :] for h in range(2)]
            hid[1 + v // ANG, v % ANG, 2 * p * middle:(2 * p + 2) * middle, :] = (
                jnp.concatenate(both, axis=0).astype(BF16))
        sent.append(view_copies(hid, p, slice(2 * p * middle, (2 * p + 2) * middle)))
    for copy in weights[3]:
        copy.wait()

    def partial(ref, u, q, near):
        lo, hi = max(2 * q - 1, 0), min(2 * q + 3, ANG)
        first, last = lo - (2 * q - 1), hi - (2 * q - 1)
        lhs, rhs = [], []
        for a in range(3):
            if (1 <= u + a <= grid_rows) != near:
                continue
            lhs.extend(ref[u + a, v] for v in range(lo, hi))
            rhs.append(awide[a, first:last].reshape((last - first) * chans, 2 * chans))
        return jnp.dot(jnp.concatenate(lhs, axis=1), jnp.concatenate(rhs, axis=0), preferred_element_type=F32)

    blocks = [(u, q) for u in range(grid_rows) for q in range(ANG // 2)]

    def finish(ref, sums, put):
        for u, q in blocks:
            total = sums[u, q]
            if u == 0 or u == grid_rows - 1:
                total = total + partial(ref, u, q, False)
            for h in range(2):
                value = total[:, h * chans:(h + 1) * chans] + ao[...]
                for r in range(rows):
                    put(u * ANG + 2 * q + h, r, value)

    def put_middle(v, r, value):
        full[v, r * cols + EDGE:(r + 1) * cols - EDGE, :] = value[r * middle:(r + 1) * middle]

    def put_edge(v, r, value):
        start = 2 * EDGE * r
        full[v, r * cols:r * cols + EDGE, :] = value[start:start + EDGE]
        full[v, (r + 1) * cols - EDGE:(r + 1) * cols, :] = value[start + EDGE:start + 2 * EDGE]

    for u, q in blocks:
        acc[u, q] = partial(hid, u, q, True)

    to_left.wait()
    to_right.wait()
    store_outer(x1, outer(0, x0, ((0, 3), (cols + 1, cols + 4))), cols + 4)
    store_outer(x2, outer(1, x1, ((0, 3), (cols - 1, cols + 2))), cols + 2)
    span = 2 * EDGE * views
    for h, value in enumerate(outer(2, x2, ((0, EDGE), (cols - EDGE, cols)))):
        for p in range(pairs):
            flip_edge[2 * p + h] = value[p * span:(p + 1) * span]
    for v in range(views):
        for p in range(pairs):
            both = [flip_edge[2 * p + h, pl.ds(v, 2 * EDGE, stride=views), :] for h in range(2)]
            hid_edge[1 + v // ANG, v % ANG, 4 * EDGE * p:4 * EDGE * (p + 1), :] = (
                jnp.concatenate(both, axis=0).astype(BF16))
    last_sent = view_copies(hid_edge, pairs, slice(0, 2 * EDGE * rows))

    receive(sent)
    finish(hid, acc, put_middle)
    for u, q in blocks:
        acc_edge[u, q] = partial(hid_edge, u, q, True)
    receive([last_sent])
    finish(hid_edge, acc_edge, put_edge)
    for v in range(views):
        out[v] = full[v].astype(BF16).reshape(rows, cols, chans)

    @pl.when(has_high)
    def _():
        for up, _ in sent + [last_sent]:
            up.wait_send()

    @pl.when(has_low)
    def _():
        for _, down in sent + [last_sent]:
            down.wait_send()


def local(lon_count, view_count, lf, sw, so, aw, ao):
    views, rows, cols, chans = lf.shape
    layers = sw.shape[0]
    grid_rows = views // ANG
    pairs = rows // 2
    hbm = pl.BlockSpec(memory_space=pltpu.HBM)
    vmem = pl.BlockSpec(memory_space=pltpu.VMEM)
    angular = pl.pallas_call(
        functools.partial(kernel, lon_count, view_count),
        out_shape=jax.ShapeDtypeStruct(lf.shape, BF16),
        in_specs=[hbm] * 5,
        out_specs=vmem,
        scratch_shapes=[
            pltpu.VMEM(so.shape, F32),
            pltpu.VMEM((1, chans), F32),
            pltpu.VMEM(lf.shape, BF16),
            pltpu.VMEM((rows + 2, (cols + 6) * views, chans), BF16),
            pltpu.VMEM((rows + 2, (cols + 4) * views, chans), BF16),
            pltpu.VMEM((rows + 2, (cols + 2) * views, chans), BF16),
            pltpu.VMEM((rows, cols * views, chans), F32),
            pltpu.VMEM((rows, 2 * EDGE * views, chans), F32),
            pltpu.VMEM((grid_rows + 2, ANG, rows * (cols - 2 * EDGE), chans), BF16),
            pltpu.VMEM((grid_rows + 2, ANG, rows * 2 * EDGE, chans), BF16),
            pltpu.VMEM((layers, 4, 3, chans, 2 * chans), BF16),
            pltpu.VMEM((3, 4, chans, 2 * chans), BF16),
            pltpu.VMEM((grid_rows, ANG // 2, rows * (cols - 2 * EDGE), 2 * chans), F32),
            pltpu.VMEM((grid_rows, ANG // 2, rows * 2 * EDGE, 2 * chans), F32),
            pltpu.VMEM((views, rows * cols, chans), F32),
            pltpu.SemaphoreType.DMA((rows,)),
            pltpu.SemaphoreType.DMA((layers + 1, 2)),
            pltpu.SemaphoreType.DMA((2,)),
            pltpu.SemaphoreType.DMA((2,)),
            pltpu.SemaphoreType.DMA((2,)),
            pltpu.SemaphoreType.DMA((2, pairs + 1)),
            pltpu.SemaphoreType.DMA((2, pairs + 1)),
        ],
        compiler_params=pltpu.CompilerParams(collective_id=0, has_side_effects=True, vmem_limit_bytes=60 * 1024 * 1024),
    )(lf, sw, so, aw, ao.reshape(1, chans))
    return (lf.astype(F32) + angular.astype(F32)).astype(BF16)


def solution(mesh):
    return jax.shard_map(
        functools.partial(local, mesh.shape["lon"], mesh.shape["view"]),
        mesh=mesh,
        in_specs=(P(("grp", "view"), None, "lon", None), P(), P(), P(), P()),
        out_specs=P(("grp", "view"), None, "lon", None),
        check_vma=False,
    )
```

```python
import functools

import jax
import jax.numpy as jnp
from jax import lax
from jax.experimental import pallas as pl
from jax.experimental.pallas import tpu as pltpu
from jax.sharding import PartitionSpec as P

ANG = 8
EDGE = 4
F32 = jnp.float32
BF16 = jnp.bfloat16


def gelu(t):
    return 0.5 * t * (1.0 + jnp.tanh(0.7978845608 * (t + 0.044715 * (t * t * t))))


def kernel(lon_count, view_count, lf, sw, so_hbm, aw, ao_hbm, out, so, ao, lfv, x0, x1, x2, flip, flip_edge, hid, hid_edge, wide, awide,
           acc, acc_edge, full,
           in_sem, w_sem, b_sem, lon_send, lon_recv, view_send, view_recv):
    views, rows, cols, chans = lf.shape
    layers = sw.shape[0]
    grid_rows = views // ANG
    pairs = rows // 2
    lon = lax.axis_index("lon")
    view = lax.axis_index("view")
    right, left = lax.rem(lon + 1, lon_count), lax.rem(lon + lon_count - 1, lon_count)
    has_low, has_high = view > 0, view < view_count - 1

    barrier = pltpu.get_barrier_semaphore()
    for neighbour in (left, right):
        pl.semaphore_signal(barrier, inc=1, device_id={"lon": neighbour}, device_id_type=pl.DeviceIdType.MESH)

    @pl.when(has_low)
    def _():
        pl.semaphore_signal(barrier, inc=1, device_id={"view": view - 1}, device_id_type=pl.DeviceIdType.MESH)

    @pl.when(has_high)
    def _():
        pl.semaphore_signal(barrier, inc=1, device_id={"view": view + 1}, device_id_type=pl.DeviceIdType.MESH)

    loads = [pltpu.make_async_copy(lf.at[:, r], lfv.at[:, r], in_sem.at[r]) for r in range(rows)]
    for load in loads:
        load.start()
    biases = [pltpu.make_async_copy(so_hbm, so, b_sem.at[0]), pltpu.make_async_copy(ao_hbm, ao, b_sem.at[1])]
    for copy in biases:
        copy.start()
    weights = []
    for l in range(layers):
        weights.append((
            pltpu.make_async_copy(sw.at[l], wide.at[l, 0:3, :, :, 0:chans], w_sem.at[l, 0]),
            pltpu.make_async_copy(sw.at[l], wide.at[l, 1:4, :, :, chans:2 * chans], w_sem.at[l, 1]),
        ))
    weights.append((
        pltpu.make_async_copy(aw, awide.at[:, 0:3, :, 0:chans], w_sem.at[layers, 0]),
        pltpu.make_async_copy(aw, awide.at[:, 1:4, :, chans:2 * chans], w_sem.at[layers, 1]),
    ))
    for both in weights:
        for copy in both:
            copy.start()

    blank = jnp.zeros((3, chans, chans), BF16)
    for l in range(layers):
        wide[l, 0, :, :, chans:2 * chans] = blank
        wide[l, 3, :, :, 0:chans] = blank
    awide[:, 0, :, chans:2 * chans] = blank
    awide[:, 3, :, 0:chans] = blank

    @pl.when(jnp.logical_not(has_low))
    def _():
        hid[0] = jnp.zeros(hid.shape[1:], BF16)
        hid_edge[0] = jnp.zeros(hid_edge.shape[1:], BF16)

    @pl.when(jnp.logical_not(has_high))
    def _():
        hid[grid_rows + 1] = jnp.zeros(hid.shape[1:], BF16)
        hid_edge[grid_rows + 1] = jnp.zeros(hid_edge.shape[1:], BF16)

    for x in (x0, x1, x2):
        x[0] = jnp.zeros(x.shape[1:], BF16)
        x[rows + 1] = jnp.zeros(x.shape[1:], BF16)

    for r in range(rows):
        loads[r].wait()
        for v in range(views):
            flip[r, pl.ds(v, cols, stride=views), :] = lfv[v, r].astype(F32)
        x0[r + 1, 3 * views:(cols + 3) * views, :] = flip[r].astype(BF16)

    def activate(l, total):
        offset = so[l:l + 1, :]
        return [gelu(total[:, h * chans:(h + 1) * chans] + offset) for h in range(2)]

    def inner(l, src, p, start, end):
        low, high = max(2 * p, 1), min(2 * p + 4, rows + 1)
        first, last = low - 2 * p, high - 2 * p
        taps = [src[row, (start + b) * views:(end + b) * views, :] for row in range(low, high) for b in range(3)]
        weight = wide[l, first:last].reshape((last - first) * 3 * chans, 2 * chans)
        return activate(l, jnp.dot(jnp.concatenate(taps, axis=1), weight, preferred_element_type=F32))

    def outer(l, src, spans):
        taps = []
        for i in range(4):
            for b in range(3):
                taps.append(jnp.concatenate(
                    [src[2 * p + i, (s + b) * views:(e + b) * views, :] for p in range(pairs) for s, e in spans], axis=0))
        weight = wide[l].reshape(12 * chans, 2 * chans)
        return activate(l, jnp.dot(jnp.concatenate(taps, axis=1), weight, preferred_element_type=F32))

    def store_outer(dst, values, width):
        side = 3 * views
        for h, value in enumerate(values):
            value = value.astype(BF16)
            for p in range(pairs):
                dst[2 * p + h + 1, 0:side, :] = value[2 * p * side:(2 * p + 1) * side]
                dst[2 * p + h + 1, (width - 3) * views:width * views, :] = value[(2 * p + 1) * side:(2 * p + 2) * side]

    def view_copies(ref, k, span):
        up = pltpu.make_async_remote_copy(
            src_ref=ref.at[grid_rows, :, span], dst_ref=ref.at[0, :, span],
            send_sem=view_send.at[0, k], recv_sem=view_recv.at[0, k],
            device_id={"view": view + 1}, device_id_type=pl.DeviceIdType.MESH)
        down = pltpu.make_async_remote_copy(
            src_ref=ref.at[1, :, span], dst_ref=ref.at[grid_rows + 1, :, span],
            send_sem=view_send.at[1, k], recv_sem=view_recv.at[1, k],
            device_id={"view": view - 1}, device_id_type=pl.DeviceIdType.MESH)

        @pl.when(has_high)
        def _():
            up.start()

        @pl.when(has_low)
        def _():
            down.start()

        return up, down

    def receive(copies):
        @pl.when(has_low)
        def _():
            for up, _ in copies:
                up.wait_recv()

        @pl.when(has_high)
        def _():
            for _, down in copies:
                down.wait_recv()

    pl.semaphore_wait(barrier, 2 + has_low.astype(jnp.int32) + has_high.astype(jnp.int32))
    to_left = pltpu.make_async_remote_copy(
        src_ref=x0.at[1:rows + 1, 3 * views:6 * views],
        dst_ref=x0.at[1:rows + 1, (cols + 3) * views:(cols + 6) * views],
        send_sem=lon_send.at[0], recv_sem=lon_recv.at[0],
        device_id={"lon": left}, device_id_type=pl.DeviceIdType.MESH)
    to_right = pltpu.make_async_remote_copy(
        src_ref=x0.at[1:rows + 1, cols * views:(cols + 3) * views], dst_ref=x0.at[1:rows + 1, 0:3 * views],
        send_sem=lon_send.at[1], recv_sem=lon_recv.at[1],
        device_id={"lon": right}, device_id_type=pl.DeviceIdType.MESH)
    to_left.start()
    to_right.start()

    for copy in biases:
        copy.wait()
    for copy in weights[0]:
        copy.wait()
    for p in range(pairs):
        for h, value in enumerate(inner(0, x0, p, 3, cols + 1)):
            x1[2 * p + h + 1, 3 * views:(cols + 1) * views, :] = value.astype(BF16)
    for copy in weights[1]:
        copy.wait()
    for p in range(pairs):
        for h, value in enumerate(inner(1, x1, p, 3, cols - 1)):
            x2[2 * p + h + 1, 3 * views:(cols - 1) * views, :] = value.astype(BF16)

    for copy in weights[2]:
        copy.wait()
    middle = cols - 2 * EDGE
    sent = []
    for p in range(pairs):
        for h, value in enumerate(inner(2, x2, p, EDGE, cols - EDGE)):
            flip[2 * p + h, 0:middle * views] = value
        for v in range(views):
            both = [flip[2 * p + h, pl.ds(v, middle, stride=views), :] for h in range(2)]
            hid[1 + v // ANG, v % ANG, 2 * p * middle:(2 * p + 2) * middle, :] = (
                jnp.concatenate(both, axis=0).astype(BF16))
        sent.append(view_copies(hid, p, slice(2 * p * middle, (2 * p + 2) * middle)))
    for copy in weights[3]:
        copy.wait()

    def partial(ref, u, q, near):
        lo, hi = max(2 * q - 1, 0), min(2 * q + 3, ANG)
        first, last = lo - (2 * q - 1), hi - (2 * q - 1)
        lhs, rhs = [], []
        for a in range(3):
            if (1 <= u + a <= grid_rows) != near:
                continue
            lhs.extend(ref[u + a, v] for v in range(lo, hi))
            rhs.append(awide[a, first:last].reshape((last - first) * chans, 2 * chans))
        return jnp.dot(jnp.concatenate(lhs, axis=1), jnp.concatenate(rhs, axis=0), preferred_element_type=F32)

    blocks = [(u, q) for u in range(grid_rows) for q in range(ANG // 2)]

    def finish(ref, sums, put):
        for u, q in blocks:
            total = sums[u, q]
            if u == 0 or u == grid_rows - 1:
                total = total + partial(ref, u, q, False)
            for h in range(2):
                value = total[:, h * chans:(h + 1) * chans] + ao[...]
                for r in range(rows):
                    put(u * ANG + 2 * q + h, r, value)

    def put_middle(v, r, value):
        full[v, r * cols + EDGE:(r + 1) * cols - EDGE, :] = value[r * middle:(r + 1) * middle]

    def put_edge(v, r, value):
        start = 2 * EDGE * r
        full[v, r * cols:r * cols + EDGE, :] = value[start:start + EDGE]
        full[v, (r + 1) * cols - EDGE:(r + 1) * cols, :] = value[start + EDGE:start + 2 * EDGE]

    for u, q in blocks:
        acc[u, q] = partial(hid, u, q, True)

    to_left.wait()
    to_right.wait()
    store_outer(x1, outer(0, x0, ((0, 3), (cols + 1, cols + 4))), cols + 4)
    store_outer(x2, outer(1, x1, ((0, 3), (cols - 1, cols + 2))), cols + 2)
    span = 2 * EDGE * views
    for h, value in enumerate(outer(2, x2, ((0, EDGE), (cols - EDGE, cols)))):
        for p in range(pairs):
            flip_edge[2 * p + h] = value[p * span:(p + 1) * span]
    for v in range(views):
        for p in range(pairs):
            both = [flip_edge[2 * p + h, pl.ds(v, 2 * EDGE, stride=views), :] for h in range(2)]
            hid_edge[1 + v // ANG, v % ANG, 4 * EDGE * p:4 * EDGE * (p + 1), :] = (
                jnp.concatenate(both, axis=0).astype(BF16))
    last_sent = view_copies(hid_edge, pairs, slice(0, 2 * EDGE * rows))

    receive(sent)
    finish(hid, acc, put_middle)
    for u, q in blocks:
        acc_edge[u, q] = partial(hid_edge, u, q, True)
    receive([last_sent])
    finish(hid_edge, acc_edge, put_edge)
    for v in range(views):
        out[v] = full[v].astype(BF16).reshape(rows, cols, chans)

    @pl.when(has_high)
    def _():
        for up, _ in sent + [last_sent]:
            up.wait_send()

    @pl.when(has_low)
    def _():
        for _, down in sent + [last_sent]:
            down.wait_send()


def local(lon_count, view_count, lf, sw, so, aw, ao):
    views, rows, cols, chans = lf.shape
    layers = sw.shape[0]
    grid_rows = views // ANG
    pairs = rows // 2
    hbm = pl.BlockSpec(memory_space=pltpu.HBM)
    vmem = pl.BlockSpec(memory_space=pltpu.VMEM)
    angular = pl.pallas_call(
        functools.partial(kernel, lon_count, view_count),
        out_shape=jax.ShapeDtypeStruct(lf.shape, BF16),
        in_specs=[hbm] * 5,
        out_specs=vmem,
        scratch_shapes=[
            pltpu.VMEM(so.shape, F32),
            pltpu.VMEM((1, chans), F32),
            pltpu.VMEM(lf.shape, BF16),
            pltpu.VMEM((rows + 2, (cols + 6) * views, chans), BF16),
            pltpu.VMEM((rows + 2, (cols + 4) * views, chans), BF16),
            pltpu.VMEM((rows + 2, (cols + 2) * views, chans), BF16),
            pltpu.VMEM((rows, cols * views, chans), F32),
            pltpu.VMEM((rows, 2 * EDGE * views, chans), F32),
            pltpu.VMEM((grid_rows + 2, ANG, rows * (cols - 2 * EDGE), chans), BF16),
            pltpu.VMEM((grid_rows + 2, ANG, rows * 2 * EDGE, chans), BF16),
            pltpu.VMEM((layers, 4, 3, chans, 2 * chans), BF16),
            pltpu.VMEM((3, 4, chans, 2 * chans), BF16),
            pltpu.VMEM((grid_rows, ANG // 2, rows * (cols - 2 * EDGE), 2 * chans), F32),
            pltpu.VMEM((grid_rows, ANG // 2, rows * 2 * EDGE, 2 * chans), F32),
            pltpu.VMEM((views, rows * cols, chans), F32),
            pltpu.SemaphoreType.DMA((rows,)),
            pltpu.SemaphoreType.DMA((layers + 1, 2)),
            pltpu.SemaphoreType.DMA((2,)),
            pltpu.SemaphoreType.DMA((2,)),
            pltpu.SemaphoreType.DMA((2,)),
            pltpu.SemaphoreType.DMA((2, pairs + 1)),
            pltpu.SemaphoreType.DMA((2, pairs + 1)),
        ],
        compiler_params=pltpu.CompilerParams(collective_id=0, has_side_effects=True, vmem_limit_bytes=60 * 1024 * 1024),
    )(lf, sw, so, aw, ao.reshape(1, chans))
    return (lf.astype(F32) + angular.astype(F32)).astype(BF16)


def solution(mesh):
    return jax.shard_map(
        functools.partial(local, mesh.shape["lon"], mesh.shape["view"]),
        mesh=mesh,
        in_specs=(P(("grp", "view"), None, "lon", None), P(), P(), P(), P()),
        out_specs=P(("grp", "view"), None, "lon", None),
        check_vma=False,
    )
```

```python
import functools

import jax
import jax.numpy as jnp
from jax import lax
from jax.experimental import pallas as pl
from jax.experimental.pallas import tpu as pltpu
from jax.sharding import PartitionSpec as P

ANG = 8
EDGE = 4
F32 = jnp.float32
BF16 = jnp.bfloat16


def gelu(t):
    return 0.5 * t * (1.0 + jnp.tanh(0.7978845608 * (t + 0.044715 * (t * t * t))))


def kernel(lon_count, view_count, lf, sw, so_hbm, aw, ao_hbm, out, so, ao, lfv, x0, x1, x2, flip, flip_edge, hid, hid_edge, wide, awide,
           acc, acc_edge, full,
           in_sem, w_sem, b_sem, lon_send, lon_recv, view_send, view_recv):
    views, rows, cols, chans = lf.shape
    layers = sw.shape[0]
    grid_rows = views // ANG
    pairs = rows // 2
    lon = lax.axis_index("lon")
    view = lax.axis_index("view")
    right, left = lax.rem(lon + 1, lon_count), lax.rem(lon + lon_count - 1, lon_count)
    has_low, has_high = view > 0, view < view_count - 1

    barrier = pltpu.get_barrier_semaphore()
    for neighbour in (left, right):
        pl.semaphore_signal(barrier, inc=1, device_id={"lon": neighbour}, device_id_type=pl.DeviceIdType.MESH)

    @pl.when(has_low)
    def _():
        pl.semaphore_signal(barrier, inc=1, device_id={"view": view - 1}, device_id_type=pl.DeviceIdType.MESH)

    @pl.when(has_high)
    def _():
        pl.semaphore_signal(barrier, inc=1, device_id={"view": view + 1}, device_id_type=pl.DeviceIdType.MESH)

    loads = [pltpu.make_async_copy(lf.at[:, r], lfv.at[:, r], in_sem.at[r]) for r in range(rows)]
    for load in loads:
        load.start()
    biases = [pltpu.make_async_copy(so_hbm, so, b_sem.at[0]), pltpu.make_async_copy(ao_hbm, ao, b_sem.at[1])]
    for copy in biases:
        copy.start()
    weights = []
    for l in range(layers):
        weights.append((
            pltpu.make_async_copy(sw.at[l], wide.at[l, 0:3, :, :, 0:chans], w_sem.at[l, 0]),
            pltpu.make_async_copy(sw.at[l], wide.at[l, 1:4, :, :, chans:2 * chans], w_sem.at[l, 1]),
        ))
    weights.append((
        pltpu.make_async_copy(aw, awide.at[:, 0:3, :, 0:chans], w_sem.at[layers, 0]),
        pltpu.make_async_copy(aw, awide.at[:, 1:4, :, chans:2 * chans], w_sem.at[layers, 1]),
    ))
    for both in weights:
        for copy in both:
            copy.start()

    blank = jnp.zeros((3, chans, chans), BF16)
    for l in range(layers):
        wide[l, 0, :, :, chans:2 * chans] = blank
        wide[l, 3, :, :, 0:chans] = blank
    awide[:, 0, :, chans:2 * chans] = blank
    awide[:, 3, :, 0:chans] = blank

    @pl.when(jnp.logical_not(has_low))
    def _():
        hid[0] = jnp.zeros(hid.shape[1:], BF16)
        hid_edge[0] = jnp.zeros(hid_edge.shape[1:], BF16)

    @pl.when(jnp.logical_not(has_high))
    def _():
        hid[grid_rows + 1] = jnp.zeros(hid.shape[1:], BF16)
        hid_edge[grid_rows + 1] = jnp.zeros(hid_edge.shape[1:], BF16)

    for x in (x0, x1, x2):
        x[0] = jnp.zeros(x.shape[1:], BF16)
        x[rows + 1] = jnp.zeros(x.shape[1:], BF16)

    for r in range(rows):
        loads[r].wait()
        for v in range(views):
            flip[r, pl.ds(v, cols, stride=views), :] = lfv[v, r].astype(F32)
        x0[r + 1, 3 * views:(cols + 3) * views, :] = flip[r].astype(BF16)

    def activate(l, total):
        offset = so[l:l + 1, :]
        return [gelu(total[:, h * chans:(h + 1) * chans] + offset) for h in range(2)]

    def inner(l, src, p, start, end):
        low, high = max(2 * p, 1), min(2 * p + 4, rows + 1)
        first, last = low - 2 * p, high - 2 * p
        taps = [src[row, (start + b) * views:(end + b) * views, :] for row in range(low, high) for b in range(3)]
        weight = wide[l, first:last].reshape((last - first) * 3 * chans, 2 * chans)
        return activate(l, jnp.dot(jnp.concatenate(taps, axis=1), weight, preferred_element_type=F32))

    def outer(l, src, spans):
        taps = []
        for i in range(4):
            for b in range(3):
                taps.append(jnp.concatenate(
                    [src[2 * p + i, (s + b) * views:(e + b) * views, :] for p in range(pairs) for s, e in spans], axis=0))
        weight = wide[l].reshape(12 * chans, 2 * chans)
        return activate(l, jnp.dot(jnp.concatenate(taps, axis=1), weight, preferred_element_type=F32))

    def store_outer(dst, values, width):
        side = 3 * views
        for h, value in enumerate(values):
            value = value.astype(BF16)
            for p in range(pairs):
                dst[2 * p + h + 1, 0:side, :] = value[2 * p * side:(2 * p + 1) * side]
                dst[2 * p + h + 1, (width - 3) * views:width * views, :] = value[(2 * p + 1) * side:(2 * p + 2) * side]

    def view_copies(ref, k, span):
        up = pltpu.make_async_remote_copy(
            src_ref=ref.at[grid_rows, :, span], dst_ref=ref.at[0, :, span],
            send_sem=view_send.at[0, k], recv_sem=view_recv.at[0, k],
            device_id={"view": view + 1}, device_id_type=pl.DeviceIdType.MESH)
        down = pltpu.make_async_remote_copy(
            src_ref=ref.at[1, :, span], dst_ref=ref.at[grid_rows + 1, :, span],
            send_sem=view_send.at[1, k], recv_sem=view_recv.at[1, k],
            device_id={"view": view - 1}, device_id_type=pl.DeviceIdType.MESH)

        @pl.when(has_high)
        def _():
            up.start()

        @pl.when(has_low)
        def _():
            down.start()

        return up, down

    def receive(copies):
        @pl.when(has_low)
        def _():
            for up, _ in copies:
                up.wait_recv()

        @pl.when(has_high)
        def _():
            for _, down in copies:
                down.wait_recv()

    pl.semaphore_wait(barrier, 2 + has_low.astype(jnp.int32) + has_high.astype(jnp.int32))
    to_left = pltpu.make_async_remote_copy(
        src_ref=x0.at[1:rows + 1, 3 * views:6 * views],
        dst_ref=x0.at[1:rows + 1, (cols + 3) * views:(cols + 6) * views],
        send_sem=lon_send.at[0], recv_sem=lon_recv.at[0],
        device_id={"lon": left}, device_id_type=pl.DeviceIdType.MESH)
    to_right = pltpu.make_async_remote_copy(
        src_ref=x0.at[1:rows + 1, cols * views:(cols + 3) * views], dst_ref=x0.at[1:rows + 1, 0:3 * views],
        send_sem=lon_send.at[1], recv_sem=lon_recv.at[1],
        device_id={"lon": right}, device_id_type=pl.DeviceIdType.MESH)
    to_left.start()
    to_right.start()

    for copy in biases:
        copy.wait()
    for copy in weights[0]:
        copy.wait()
    for p in range(pairs):
        for h, value in enumerate(inner(0, x0, p, 3, cols + 1)):
            x1[2 * p + h + 1, 3 * views:(cols + 1) * views, :] = value.astype(BF16)
    for copy in weights[1]:
        copy.wait()
    for p in range(pairs):
        for h, value in enumerate(inner(1, x1, p, 3, cols - 1)):
            x2[2 * p + h + 1, 3 * views:(cols - 1) * views, :] = value.astype(BF16)

    for copy in weights[2]:
        copy.wait()
    middle = cols - 2 * EDGE
    sent = []
    for p in range(pairs):
        for h, value in enumerate(inner(2, x2, p, EDGE, cols - EDGE)):
            flip[2 * p + h, 0:middle * views] = value
        for v in range(views):
            both = [flip[2 * p + h, pl.ds(v, middle, stride=views), :] for h in range(2)]
            hid[1 + v // ANG, v % ANG, 2 * p * middle:(2 * p + 2) * middle, :] = (
                jnp.concatenate(both, axis=0).astype(BF16))
        sent.append(view_copies(hid, p, slice(2 * p * middle, (2 * p + 2) * middle)))
    for copy in weights[3]:
        copy.wait()

    def partial(ref, u, q, near):
        lo, hi = max(2 * q - 1, 0), min(2 * q + 3, ANG)
        first, last = lo - (2 * q - 1), hi - (2 * q - 1)
        lhs, rhs = [], []
        for a in range(3):
            if (1 <= u + a <= grid_rows) != near:
                continue
            lhs.extend(ref[u + a, v] for v in range(lo, hi))
            rhs.append(awide[a, first:last].reshape((last - first) * chans, 2 * chans))
        return jnp.dot(jnp.concatenate(lhs, axis=1), jnp.concatenate(rhs, axis=0), preferred_element_type=F32)

    blocks = [(u, q) for u in range(grid_rows) for q in range(ANG // 2)]

    def finish(ref, sums, put):
        for u, q in blocks:
            total = sums[u, q]
            if u == 0 or u == grid_rows - 1:
                total = total + partial(ref, u, q, False)
            for h in range(2):
                value = total[:, h * chans:(h + 1) * chans] + ao[...]
                for r in range(rows):
                    put(u * ANG + 2 * q + h, r, value)

    def put_middle(v, r, value):
        full[v, r * cols + EDGE:(r + 1) * cols - EDGE, :] = value[r * middle:(r + 1) * middle]

    def put_edge(v, r, value):
        start = 2 * EDGE * r
        full[v, r * cols:r * cols + EDGE, :] = value[start:start + EDGE]
        full[v, (r + 1) * cols - EDGE:(r + 1) * cols, :] = value[start + EDGE:start + 2 * EDGE]

    for u, q in blocks:
        acc[u, q] = partial(hid, u, q, True)

    to_left.wait()
    to_right.wait()
    store_outer(x1, outer(0, x0, ((0, 3), (cols + 1, cols + 4))), cols + 4)
    store_outer(x2, outer(1, x1, ((0, 3), (cols - 1, cols + 2))), cols + 2)
    span = 2 * EDGE * views
    for h, value in enumerate(outer(2, x2, ((0, EDGE), (cols - EDGE, cols)))):
        for p in range(pairs):
            flip_edge[2 * p + h] = value[p * span:(p + 1) * span]
    for v in range(views):
        for p in range(pairs):
            both = [flip_edge[2 * p + h, pl.ds(v, 2 * EDGE, stride=views), :] for h in range(2)]
            hid_edge[1 + v // ANG, v % ANG, 4 * EDGE * p:4 * EDGE * (p + 1), :] = (
                jnp.concatenate(both, axis=0).astype(BF16))
    last_sent = view_copies(hid_edge, pairs, slice(0, 2 * EDGE * rows))

    for u, q in blocks:
        acc_edge[u, q] = partial(hid_edge, u, q, True)
    receive(sent)
    finish(hid, acc, put_middle)
    receive([last_sent])
    finish(hid_edge, acc_edge, put_edge)
    for v in range(views):
        out[v] = full[v].astype(BF16).reshape(rows, cols, chans)

    @pl.when(has_high)
    def _():
        for up, _ in sent + [last_sent]:
            up.wait_send()

    @pl.when(has_low)
    def _():
        for _, down in sent + [last_sent]:
            down.wait_send()


def local(lon_count, view_count, lf, sw, so, aw, ao):
    views, rows, cols, chans = lf.shape
    layers = sw.shape[0]
    grid_rows = views // ANG
    pairs = rows // 2
    hbm = pl.BlockSpec(memory_space=pltpu.HBM)
    vmem = pl.BlockSpec(memory_space=pltpu.VMEM)
    angular = pl.pallas_call(
        functools.partial(kernel, lon_count, view_count),
        out_shape=jax.ShapeDtypeStruct(lf.shape, BF16),
        in_specs=[hbm] * 5,
        out_specs=vmem,
        scratch_shapes=[
            pltpu.VMEM(so.shape, F32),
            pltpu.VMEM((1, chans), F32),
            pltpu.VMEM(lf.shape, BF16),
            pltpu.VMEM((rows + 2, (cols + 6) * views, chans), BF16),
            pltpu.VMEM((rows + 2, (cols + 4) * views, chans), BF16),
            pltpu.VMEM((rows + 2, (cols + 2) * views, chans), BF16),
            pltpu.VMEM((rows, cols * views, chans), F32),
            pltpu.VMEM((rows, 2 * EDGE * views, chans), F32),
            pltpu.VMEM((grid_rows + 2, ANG, rows * (cols - 2 * EDGE), chans), BF16),
            pltpu.VMEM((grid_rows + 2, ANG, rows * 2 * EDGE, chans), BF16),
            pltpu.VMEM((layers, 4, 3, chans, 2 * chans), BF16),
            pltpu.VMEM((3, 4, chans, 2 * chans), BF16),
            pltpu.VMEM((grid_rows, ANG // 2, rows * (cols - 2 * EDGE), 2 * chans), F32),
            pltpu.VMEM((grid_rows, ANG // 2, rows * 2 * EDGE, 2 * chans), F32),
            pltpu.VMEM((views, rows * cols, chans), F32),
            pltpu.SemaphoreType.DMA((rows,)),
            pltpu.SemaphoreType.DMA((layers + 1, 2)),
            pltpu.SemaphoreType.DMA((2,)),
            pltpu.SemaphoreType.DMA((2,)),
            pltpu.SemaphoreType.DMA((2,)),
            pltpu.SemaphoreType.DMA((2, pairs + 1)),
            pltpu.SemaphoreType.DMA((2, pairs + 1)),
        ],
        compiler_params=pltpu.CompilerParams(collective_id=0, has_side_effects=True, vmem_limit_bytes=60 * 1024 * 1024),
    )(lf, sw, so, aw, ao.reshape(1, chans))
    return (lf.astype(F32) + angular.astype(F32)).astype(BF16)


def solution(mesh):
    return jax.shard_map(
        functools.partial(local, mesh.shape["lon"], mesh.shape["view"]),
        mesh=mesh,
        in_specs=(P(("grp", "view"), None, "lon", None), P(), P(), P(), P()),
        out_specs=P(("grp", "view"), None, "lon", None),
        check_vma=False,
    )
```
